32 devices in a mesh: section: 4 (over y, x), seq: 8 (over z, core).
Axes of the slice: x: 2, y: 2, z: 4, core: 2. Of those that a mesh axis runs over, the one named last changes fastest.
Arguments:
- inputs: bfloat16 [4, 4096, 1536], P(None, 'seq'), may hold values from -40 to 40
- weights: bfloat16 [2, 5, 1536, 1536], P(None, None, None, 'section'), may hold values from -0.0625 to 0.0625
- gains: float32 [2, 1536], replicated, may hold values from 0.1 to 1.9
Outputs:
- activations: bfloat16 [2, 4, 4096, 1536], P(None, None, 'seq', 'section')
The draws below stay inside these ranges and needn't reach their ends.
All inputs are finite; a program needn't handle non-finite values.
Results may differ from the reference program's by a relative error of at most 0.0044.
Values may be sent and summed in bfloat16 or wider, within the bound.
A program may use at most 128 MiB of HBM per device.

```python
import math
import jax
import jax.numpy as jnp
from jax import lax

C = 1536
KW = 5
LAYERS = 2
MICRO = 4
LEN = 4096


def draw_inputs(key, part):
    first, second, third = jax.random.split(jax.random.fold_in(key, 11), 3)
    chan = jnp.exp(jax.random.uniform(second, (1, 1, C), jnp.float32, math.log(0.3), math.log(3.0)))
    place = jnp.exp(jax.random.uniform(third, (MICRO, LEN, 1), jnp.float32, math.log(0.3), math.log(3.0)))
    base = jnp.clip(jax.random.normal(first, (MICRO, LEN, C), jnp.float32), -4.0, 4.0)
    return (base * chan * place).astype(jnp.bfloat16)


def levels(own_key, shape, shards, least, top_value):
    level = 1.0
    for axis_at, shards_of in shards:
        heights = jax.random.uniform(jax.random.fold_in(jax.random.fold_in(own_key, 6), axis_at), (shards_of,), jnp.float32, least / len(shards), top_value / len(shards))
        level = level * jnp.repeat(jnp.exp(heights), shape[axis_at] // shards_of).reshape((-1,) + (1,) * (len(shape) - 1 - axis_at))
    return level


def centred(own_key, shape, scale, reach, cuts=(), held_as=jnp.bfloat16):
    drawn = jax.random.normal(own_key, shape, jnp.float32) * scale
    if len(cuts) > 0:
        drawn = levels(own_key, shape, cuts, -0.22, 0.18) * drawn
    return jnp.clip(drawn, min=-reach, max=reach).astype(held_as)


def setup_inputs(seed: int = 0) -> dict:
    key_list = jax.random.split(jax.random.key(seed), 4)
    inputs = draw_inputs(jax.random.fold_in(key_list[3], 71), 0)
    weights = centred(key_list[1], (LAYERS, KW, C, C), (KW * C) ** -0.5, 0.0625, ((3, 4),))
    gains = jnp.clip(1.0 + 0.18 * jax.random.normal(key_list[2], (LAYERS, C), jnp.float32), 0.1, 1.9)
    return dict(inputs=inputs, weights=weights, gains=gains)


def block(current, kernel, gain):
    values = current.astype(jnp.float32)
    scale = lax.rsqrt(lax.optimization_barrier(jnp.mean(values * values, axis=-1, keepdims=True)) + 1e-06)
    hidden = jax.nn.gelu(values * scale * gain).astype(jnp.bfloat16)
    padded = jnp.pad(hidden, ((0, 0), (2, 2), (0, 0)))
    total = jnp.zeros((MICRO * LEN, C), jnp.float32)
    for k in range(KW):
        window = padded[:, k:k + LEN, :].reshape(MICRO * LEN, C)
        total = total + jnp.dot(window, kernel[k], preferred_element_type=jnp.float32)
    return (values + total.reshape(MICRO, LEN, C)).astype(jnp.bfloat16)

def reference(inputs, weights, gains):

    def layer(current, pair):
        kernel, gain = pair
        nxt = block(current, kernel, gain)
        return (nxt, nxt)
    final, stacked = lax.scan(layer, inputs, (weights, gains))
    return stacked
```

```python
import jax
import jax.numpy as jnp
from jax import lax
from jax.experimental import pallas as pl
from jax.experimental.pallas import tpu as pltpu
from jax.sharding import PartitionSpec as P

MESH = pl.DeviceIdType.MESH
HALO = 16
REACH = 2


def with_halo(value, sides, width):
    for axis, dim in sides:
        count, length = (lax.axis_size(axis), value.shape[dim])
        up = [(i, (i + 1) % count) for i in range(count - 1)]
        down = [(j, i) for i, j in up]
        last = lax.slice_in_dim(value, length - width, length, axis=dim)
        initial = lax.slice_in_dim(value, 0, width, axis=dim)
        before = lax.ppermute(last, axis, up)
        after = lax.ppermute(initial, axis, down)
        value = jnp.concatenate([before, value, after], axis=dim)
    return value


def convolve(padded, kernel):
    count = padded.shape[1] - 4
    total = jnp.zeros((padded.shape[0], count, kernel.shape[2]), jnp.float32)
    for k in range(5):
        total = total + jnp.einsum(
            "brc,co->bro", padded[:, k : k + count], kernel[k], preferred_element_type=jnp.float32
        )
    return total


def normed(current, gain):
    values = current.astype(jnp.float32)
    scale = lax.rsqrt(jnp.mean(values * values, axis=-1, keepdims=True) + 1e-06)
    return jax.nn.gelu(values * scale * gain).astype(jnp.bfloat16)


def neighbours(hidden):
    return with_halo(hidden, (("seq", 1),), 2)


def plain(inputs, weights, gains):
    share = weights.shape[3]
    begin = lax.axis_index("section") * share
    hidden = normed(inputs, gains[0])
    conv = convolve(neighbours(hidden), weights[0])
    own = lax.dynamic_slice_in_dim(inputs, begin, share, 2)
    current = (own.astype(jnp.float32) + conv).astype(jnp.bfloat16)
    results = [current]
    kernel = weights[1]
    whole = lax.all_gather(current, "section", axis=2, tiled=True)
    conv = convolve(neighbours(normed(whole, gains[1])), kernel)
    current = (current.astype(jnp.float32) + conv).astype(jnp.bfloat16)
    results.append(current)
    return jnp.stack(results, axis=0)


def gelu(v):
    return 0.5 * v * (1.0 + jnp.tanh(0.7978845608028654 * (v + 0.044715 * (v * v * v))))


def fused_kernel(
    x, w, g, out, xe, hid, y, wv, acts, last, wsem, xsem, hsend, hrecv, ssem, rsem, osem
):
    micro, rows, chans = x.shape
    taps, share = w.shape[1], w.shape[3]
    span = rows + 2 * HALO
    half = span // 2
    part = half // 32 * 16
    me, seq = lax.axis_index("section"), lax.axis_index("seq")
    nseq = lax.axis_size("seq")

    def ring(at):
        r = at // 2
        return 2 * r + (at % 2) * (1 - 2 * (r % 2)) + r % 2

    place = ring(me)
    right, left = ring((place + 1) % 4), ring((place + 3) % 4)
    over = ring((place + 2) % 4)

    for b in range(micro):
        pltpu.make_async_copy(x.at[b], xe.at[b, pl.ds(HALO, rows)], xsem.at[b]).start()
    for l in range(2):
        for k in range(taps):
            pltpu.make_async_copy(
                w.at[l, k], wv.at[l, :, pl.ds(k * share, share)], wsem.at[l, k]
            ).start()

    barrier = pltpu.get_barrier_semaphore()
    for to in (right, left):
        pl.semaphore_signal(barrier, inc=1, device_id=(to, seq), device_id_type=MESH)

    @pl.when(seq > 0)
    def _():
        pl.semaphore_signal(barrier, inc=1, device_id=(me, seq - 1), device_id_type=MESH)

    @pl.when(seq < nseq - 1)
    def _():
        pl.semaphore_signal(barrier, inc=1, device_id=(me, seq + 1), device_id_type=MESH)

    peers = 2 + jnp.where(seq > 0, 1, 0) + jnp.where(seq < nseq - 1, 1, 0)
    pl.semaphore_wait(barrier, peers)

    def halo_up():
        return pltpu.make_async_remote_copy(
            src_ref=x.at[:, pl.ds(rows - HALO, HALO), :],
            dst_ref=xe.at[:, pl.ds(0, HALO), :],
            send_sem=hsend.at[0],
            recv_sem=hrecv.at[0],
            device_id=(me, seq + 1),
            device_id_type=MESH,
        )

    def halo_down():
        return pltpu.make_async_remote_copy(
            src_ref=x.at[:, pl.ds(0, HALO), :],
            dst_ref=xe.at[:, pl.ds(HALO + rows, HALO), :],
            send_sem=hsend.at[1],
            recv_sem=hrecv.at[1],
            device_id=(me, seq - 1),
            device_id_type=MESH,
        )

    @pl.when(seq < nseq - 1)
    def _():
        halo_up().start()

    @pl.when(seq > 0)
    def _():
        halo_down().start()

    @pl.when(seq == 0)
    def _():
        xe[:, 0:HALO, :] = jnp.zeros((micro, HALO, chans), jnp.bfloat16)

    @pl.when(seq == nseq - 1)
    def _():
        xe[:, HALO + rows : span, :] = jnp.zeros((micro, HALO, chans), jnp.bfloat16)

    for l in range(2):
        y[l, 0:8, :] = jnp.zeros((8, taps * share), jnp.float32)
        y[l, span + 8 : span + 16, :] = jnp.zeros((8, taps * share), jnp.float32)

    def piece(origin, b, start, size):
        return acts.at[origin, b, pl.ds(start, size), :]

    def send(origin, b, start, size, way, c, to):
        return pltpu.make_async_remote_copy(
            src_ref=piece(origin, b, start, size),
            dst_ref=piece(origin, b, start, size),
            send_sem=ssem.at[way, c],
            recv_sem=rsem.at[way, c],
            device_id=(to, seq),
            device_id_type=MESH,
        )

    def direct(b, h):
        c = 2 * b + h
        send(me, b, h * half, half, 0, c, right).start()
        send(me, b, h * half, half, 1, c, left).start()

    def forward(b, h):
        c = 2 * b + h
        send(left, b, h * half, half, 0, c, left).wait_recv()
        send(left, b, h * half, part, 2, c, right).start()
        send(right, b, h * half, half, 1, c, right).wait_recv()
        send(right, b, h * half + part, half - part, 3, c, left).start()

    def arrived(b, h):
        c = 2 * b + h
        send(over, b, h * half, part, 2, c, left).wait_recv()
        send(over, b, h * half + part, half - part, 3, c, right).wait_recv()

    tile = 16

    def normalize(read, l, begin, end):
        gain = g[l : l + 1, :]

        @pl.loop(0, (end - begin) // tile)
        def _(i):
            at = pl.multiple_of(begin + i * tile, tile)
            v = read(at)
            scale = lax.rsqrt(jnp.mean(v * v, axis=-1, keepdims=True) + 1e-06)
            hid[l, pl.ds(at, tile), :] = gelu(v * scale * gain).astype(jnp.bfloat16)

    def multiply(l, begin, end):
        wide = taps * share
        step = 512
        for n in range(0, wide, step):
            size = min(step, wide - n)
            y[l, begin + 8 : end + 8, n : n + size] = jnp.dot(
                hid[l, begin:end, :], wv[l, :, n : n + size], preferred_element_type=jnp.float32
            )

    def combine(l, begin, end, residual, store):
        @pl.loop(0, (end - begin) // tile)
        def _(i):
            at = pl.multiple_of(begin + i * tile, tile)
            total = None
            for k in range(taps):
                block = y[l, pl.ds(at, tile + 16), k * share : (k + 1) * share]
                term = block[8 - REACH + k : 8 - REACH + k + tile, :]
                total = term if total is None else total + term
            store(at, residual(at) + total)

    low = jnp.where(seq == 0, HALO, 0)
    high = jnp.where(seq == nseq - 1, HALO + rows, span)
    mine = pl.ds(pl.multiple_of(me * share, 128), share)

    def first(b, h):
        def read(at):
            return xe[b, pl.ds(at, tile), :].astype(jnp.float32)

        def residual(at):
            return xe[b, pl.ds(at, tile), mine].astype(jnp.float32)

        def store(at, value):
            row = at + lax.broadcasted_iota(jnp.int32, value.shape, 0)
            value = jnp.where((row >= low) & (row < high), value, 0.0)
            acts[me, b, pl.ds(at, tile), :] = value.astype(jnp.bfloat16)

        begin, end = ((0, half + HALO), (half + HALO, span))[h]
        normalize(read, 0, begin, end)
        multiply(0, begin, end)
        combine(0, h * half, h * half + half, residual, store)

    def second(b, h):
        def read(at):
            parts = [acts[s, b, pl.ds(at, tile), :].astype(jnp.float32) for s in range(4)]
            return jnp.concatenate(parts, axis=-1)

        def residual(at):
            return acts[me, b, pl.ds(at, tile), :].astype(jnp.float32)

        def store(at, value):
            last[b, pl.ds(pl.multiple_of(at - HALO, tile), tile), :] = value.astype(jnp.bfloat16)

        normalize(read, 1, h * half, h * half + half)
        multiply(1, h * half, h * half + half)
        cut = half - HALO
        begin, end = ((HALO, cut), (cut, HALO + rows))[h]
        combine(1, begin, end, residual, store)

    def out_first(b):
        return pltpu.make_async_copy(
            acts.at[me, b, pl.ds(HALO, rows), :], out.at[0, b], osem.at[0, b]
        )

    def out_last(b):
        return pltpu.make_async_copy(last.at[b], out.at[1, b], osem.at[1, b])

    def weights_ready(l):
        for k in range(taps):
            pltpu.make_async_copy(
                w.at[l, k], wv.at[l, :, pl.ds(k * share, share)], wsem.at[l, k]
            ).wait()

    @pl.loop(0, micro + 1)
    def _(b):
        @pl.when(b < micro)
        def _():
            pltpu.make_async_copy(x.at[b], xe.at[b, pl.ds(HALO, rows)], xsem.at[b]).wait()

            @pl.when(b == 0)
            def _():
                @pl.when(seq > 0)
                def _():
                    halo_up().wait_recv()

                @pl.when(seq < nseq - 1)
                def _():
                    halo_down().wait_recv()

                weights_ready(0)

            first(b, 0)
            direct(b, 0)

        @pl.when(b > 0)
        def _():
            forward(b - 1, 1)
            arrived(b - 1, 0)

            @pl.when(b == 1)
            def _():
                weights_ready(1)

            second(b - 1, 0)

        @pl.when(b < micro)
        def _():
            first(b, 1)
            direct(b, 1)
            out_first(b).start()
            forward(b, 0)

        @pl.when(b > 0)
        def _():
            arrived(b - 1, 1)
            second(b - 1, 1)
            out_last(b - 1).start()

    @pl.when(seq < nseq - 1)
    def _():
        halo_up().wait_send()

    @pl.when(seq > 0)
    def _():
        halo_down().wait_send()

    @pl.loop(0, micro)
    def _(b):
        out_first(b).wait()
        out_last(b).wait()
        for h in range(2):
            c = 2 * b + h
            send(me, b, h * half, half, 0, c, right).wait_send()
            send(me, b, h * half, half, 1, c, left).wait_send()
            send(left, b, h * half, part, 2, c, right).wait_send()
            send(right, b, h * half + part, half - part, 3, c, left).wait_send()


def fused(inputs, weights, gains):
    micro, rows, chans = inputs.shape
    layers, taps, _, share = weights.shape
    span = rows + 2 * HALO
    chunks = 2 * micro
    dma = pltpu.SemaphoreType.DMA
    hbm = pl.BlockSpec(memory_space=pltpu.HBM)
    return pl.pallas_call(
        fused_kernel,
        out_shape=jax.ShapeDtypeStruct((layers, micro, rows, share), jnp.bfloat16),
        in_specs=[hbm, hbm, pl.BlockSpec(memory_space=pltpu.VMEM)],
        out_specs=hbm,
        scratch_shapes=[
            pltpu.VMEM((micro, span, chans), jnp.bfloat16),
            pltpu.VMEM((2, span, chans), jnp.bfloat16),
            pltpu.VMEM((2, span + 16, taps * share), jnp.float32),
            pltpu.VMEM((2, chans, taps * share), jnp.bfloat16),
            pltpu.VMEM((4, micro, span, share), jnp.bfloat16),
            pltpu.VMEM((micro, rows, share), jnp.bfloat16),
            dma((2, taps)),
            dma((micro,)),
            dma((2,)),
            dma((2,)),
            dma((4, chunks)),
            dma((4, chunks)),
            dma((2, micro)),
        ],
        compiler_params=pltpu.CompilerParams(
            collective_id=0, has_side_effects=True, vmem_limit_bytes=60 * 1024 * 1024
        ),
    )(inputs, weights, gains)


def local(inputs, weights, gains):
    square = lax.axis_size("section") == 4 and weights.shape[0] == 2
    if square and weights.shape[3] % 128 == 0 and inputs.shape[1] % 32 == 0:
        return fused(inputs, weights, gains)
    return plain(inputs, weights, gains)


def solution(mesh):
    in_specs = (P(None, "seq", None), P(None, None, None, "section"), P())
    out_specs = P(None, None, "seq", "section")
    return jax.shard_map(local, mesh=mesh, in_specs=in_specs, out_specs=out_specs, check_vma=False)
```
